256 devices in a mesh: gz: 32 (over y, z_hi, core), gy: 8 (over z_lo, x).
Axes of the slice: x: 4, y: 4, z: 8 (z_hi: 4, z_lo: 2; z = z_hi * 2 + z_lo), core: 2. Of those that a mesh axis runs over, the one named last changes fastest.
Arguments:
- estimate: float32 [512, 256, 512], P('gz', 'gy'), may hold values from 0.5 to 2
- measured: float32 [4, 512, 256, 512], P(None, 'gz', 'gy'), may hold values from 0.25 to 4
- psf_z: float32 [4, 31], replicated, may hold values from 0.1 to 1
- psf_y: float32 [4, 15], replicated, may hold values from 0.1 to 1
- psf_x: float32 [4, 15], replicated, may hold values from 0.1 to 1
- extents: int32 [4, 3], replicated, may hold values from 9 to 31, as said below
- order: int32 [4], replicated, may hold values from 0 to 3, each once
Outputs:
- updated: float32 [512, 256, 512], P('gz', 'gy')
The draws below stay inside these ranges and needn't reach their ends.
Inputs may be any that keep to these rules, and one draw needn't show every extreme that they name: `extents`: every extent is odd; along z it lies in 9 to 31, along y and x in 9 to 15; in every draw some view has extent 31 along z and some view has extent 15 along y.
All inputs are finite; a program needn't handle non-finite values.
Results may differ from the reference program's by a relative error of at most 0.0001.
Values sent between devices are 32-bit elements; how exact they have to be, the bound alone decides.
No kernel may reach another device: no remote copies, remote signals or barrier semaphores. Data moves between devices by JAX's collectives and lax.ppermute only.
A program may use at most 64 MiB of HBM per device.

```python
import math
import jax
import jax.numpy as jnp
from jax import lax

NX = 512
V = 4
KZ = 31
KL = 15
NZ = 512
NY = 256


def draw_extents(key, part):
    keys = jax.random.split(jax.random.fold_in(key, 7), 5)
    radius_z = jax.random.randint(keys[0], (V,), 4, 16)
    radius_y = jax.random.randint(keys[1], (V,), 4, 8)
    radius_x = jax.random.randint(keys[2], (V,), 4, 8)
    views = jnp.arange(V, dtype=jnp.int32)
    pick_z = jax.random.randint(keys[3], (), 0, V)
    pick_y = jax.random.randint(keys[4], (), 0, V)
    radius_z = jnp.where(views == pick_z, 15, radius_z)
    radius_y = jnp.where(views == pick_y, 7, radius_y)
    radii = jnp.stack([radius_z, radius_y, radius_x], axis=1)
    return (2 * radii + 1).astype(jnp.int32)


def block_scale(own_key, dims, pieces, least, top_value):
    def one(axis_at, parts):
        heights = jax.random.uniform(jax.random.fold_in(jax.random.fold_in(own_key, 6), axis_at), (parts,), jnp.float32, least / len(pieces), top_value / len(pieces))
        return jnp.repeat(jnp.exp(heights), dims[axis_at] // parts).reshape((-1,) + (1,) * (len(dims) - axis_at - 1))

    level = one(*pieces[0])
    for cut in pieces[1:]:
        level = level * one(*cut)
    return level


def setup_inputs(seed: int = 0) -> dict:
    streams_of = jax.random.split(jax.random.key(seed), 8)
    return {
        "estimate": jnp.clip(jnp.exp(math.log(2.0) - 1.3862944 * jax.random.uniform(streams_of[0], (NZ, NY, NX), jnp.float32) ** block_scale(streams_of[0], (NZ, NY, NX), ((0, 32), (1, 8)), -0.2, 0.2)), 0.5, 2.0),
        "measured": jnp.clip(jnp.exp(math.log(4.0) - 2.7725887 * jax.random.uniform(streams_of[1], (V, NZ, NY, NX), jnp.float32) ** block_scale(streams_of[1], (V, NZ, NY, NX), ((1, 32), (2, 8)), -0.2, 0.2)), 0.25, 4.0),
        "psf_z": jnp.clip(jnp.exp(jax.random.uniform(streams_of[2], (V, KZ), jnp.float32, math.log(0.1), math.log(1.0))), 0.1, 1.0),
        "psf_y": jnp.clip(jnp.exp(jax.random.uniform(streams_of[3], (V, KL), jnp.float32, math.log(0.1), math.log(1.0))), 0.1, 1.0),
        "psf_x": jnp.clip(jnp.exp(jax.random.uniform(streams_of[4], (V, KL), jnp.float32, math.log(0.1), math.log(1.0))), 0.1, 1.0),
        "extents": draw_extents(jax.random.fold_in(streams_of[7], 71), 0),
        "order": jax.random.permutation(streams_of[6], V).astype(jnp.int32),
    }


def line_taps(profile, reach_cells, tap_reach):
    offsets = jnp.arange(2 * tap_reach + 1, dtype=jnp.int32) - tap_reach
    kept = jnp.where(jnp.abs(offsets) <= reach_cells, profile, jnp.zeros_like(profile))
    return kept / jnp.sum(kept)


def pad_axis(field, along_axis, tap_reach):
    widths = [(0, 0), (0, 0), (0, 0)]
    widths[along_axis] = (tap_reach, tap_reach)
    return jnp.pad(field, widths)


def correlate_padded(padded, weights, along_axis, tap_reach, length, flipped):
    total = None
    for offset in range(2 * tap_reach + 1):
        start = 2 * tap_reach - offset if flipped else offset
        piece = lax.slice_in_dim(padded, start, start + length, axis=along_axis)
        term = weights[offset] * piece
        total = term if total is None else total + term
    return total


def blur(field, weights_z, weights_y, weights_x, flipped):
    result = correlate_padded(pad_axis(field, 0, 15), weights_z, 0, 15, field.shape[0], flipped)
    result = correlate_padded(pad_axis(result, 1, 7), weights_y, 1, 7, field.shape[1], flipped)
    result = correlate_padded(pad_axis(result, 2, 7), weights_x, 2, 7, field.shape[2], flipped)
    return result


def reference(estimate, measured, psf_z, psf_y, psf_x, extents, order):
    current = estimate
    for position in range(V):
        view = order[position]
        radii = (extents[view] - 1) // 2
        weights_z = line_taps(psf_z[view], radii[0], 15)
        weights_y = line_taps(psf_y[view], radii[1], 7)
        weights_x = line_taps(psf_x[view], radii[2], 7)
        blurred = blur(current, weights_z, weights_y, weights_x, False)
        ratio = measured[view] / blurred
        current = current * blur(ratio, weights_z, weights_y, weights_x, True)
    return current
```

```python
import functools

import jax
import jax.numpy as jnp
from jax import lax
from jax.experimental import pallas as pl
from jax.experimental.pallas import tpu as pltpu
from jax.sharding import PartitionSpec as P

REACH_Z = 15
REACH_L = 7
F32 = jnp.float32
BF16 = jnp.bfloat16

VMEM_SPEC = pl.BlockSpec(memory_space=pltpu.VMEM)
SMEM_SPEC = pl.BlockSpec(memory_space=pltpu.SMEM)
ANY_SPEC = pl.BlockSpec(memory_space=pl.ANY)


def line_taps(profile, reach_cells, tap_reach):
    offsets = jnp.arange(2 * tap_reach + 1, dtype=jnp.int32) - tap_reach
    kept = jnp.where(jnp.abs(offsets)[None, :] <= reach_cells[:, None], profile, jnp.zeros_like(profile))
    return kept / jnp.sum(kept, axis=1, keepdims=True)


def halves(x):
    hi = x.astype(BF16)
    return hi, (x - hi.astype(F32)).astype(BF16)


def mm(a, b):
    return jnp.dot(a, b, preferred_element_type=F32)


def banded(place, tap, count):
    value = jnp.zeros(place.shape, F32)
    for k in range(count):
        value = jnp.where(place == k, tap(k), value)
    return value


def iota2(shape, dim):
    return lax.broadcasted_iota(jnp.int32, shape, dim)


def prepare_kernel(planes, rows, reach, wz_ref, wy_ref, wx_ref, par_ref, z_ref, ye_ref, ym_ref, x_ref):
    pos = pl.program_id(0)
    flip = pl.program_id(1)
    par = par_ref[0]

    def tap_of(ref, count):
        return lambda k: ref[pos, jnp.where(flip == 1, count - 1 - k, k)]

    tall = 8 * planes
    wide = z_ref.shape[-1]

    def z_rows(chunk, carry):
        base = pl.multiple_of(chunk * 16, 16)
        r = iota2((16, wide), 0) + base
        c = iota2((16, wide), 1)
        plane = c >> 3
        second = plane >= planes + reach
        q = jnp.where(second, plane - planes - reach, plane - planes)
        below = jnp.where(second, 1 - par, par) == 1
        i = jnp.where(plane < planes, plane, jnp.where(below, q - reach, planes + q))
        d = i - (r >> 3) + REACH_Z
        d = jnp.where((r & 7) == (c & 7), d, -1)
        hi, lo = halves(banded(d, tap_of(wz_ref, 2 * REACH_Z + 1), 2 * REACH_Z + 1))
        z_ref[0, 0, pl.ds(base, 16), :] = hi
        z_ref[0, 0, pl.ds(tall + base, 16), :] = lo
        return carry

    lax.fori_loop(0, tall // 16, z_rows, 0)

    tap_y = tap_of(wy_ref, 2 * REACH_L + 1)
    tap_x = tap_of(wx_ref, 2 * REACH_L + 1)
    half = rows // 2
    r = iota2((64, 192), 0)
    c = iota2((64, 192), 1)
    zc = jnp.where(c >= 144, 3, jnp.where(c >= 96, 2, jnp.where(c >= 48, 1, 0)))
    e = r & 15
    yo = jnp.where(e < 8, e, e + half)
    d = (c - 48 * zc - 8) - yo + REACH_L
    hi, lo = halves(banded(jnp.where((r >> 4) == zc, d, -1), tap_y, 2 * REACH_L + 1))
    ye_ref[0, 0, :64, :] = hi
    ye_ref[0, 0, 64:, :] = lo
    r = iota2((128, 256), 0)
    c = iota2((128, 256), 1)
    d = (c & 31) - ((r & 15) + 8) + REACH_L
    hi, lo = halves(banded(jnp.where((r >> 4) == (c >> 5), d, -1), tap_y, 2 * REACH_L + 1))
    ym_ref[0, 0, :128, :] = hi
    ym_ref[0, 0, 128:, :] = lo

    blocks = x_ref.shape[-1] // 128
    d = iota2((128, 128), 0) - iota2((128, 128), 1) + REACH_L
    for shift in (-1, 0, 1):
        hi, lo = halves(banded(d + 128 * shift, tap_x, 2 * REACH_L + 1))
        for b in range(blocks):
            a = b + shift
            if 0 <= a < blocks:
                x_ref[0, 0, 0, 128 * a:128 * a + 128, 128 * b:128 * b + 128] = hi
                x_ref[0, 0, 1, 128 * a:128 * a + 128, 128 * b:128 * b + 128] = lo
    zero = jnp.zeros((128, 128), BF16)
    for a in range(blocks):
        for b in range(blocks):
            if abs(a - b) > 1:
                x_ref[0, 0, 0, 128 * a:128 * a + 128, 128 * b:128 * b + 128] = zero
                x_ref[0, 0, 1, 128 * a:128 * a + 128, 128 * b:128 * b + 128] = zero


def prepare(wz, wy, wx, parity, planes, rows, width, reach):
    views = wz.shape[0]
    wide = 8 * (planes + 2 * reach)

    def spec(*block):
        return pl.BlockSpec((1, 1) + block, lambda p, d: (p, d) + (0,) * len(block))

    shapes = ((16 * planes, wide), (128, 192), (256, 256), (2, width, width))
    return pl.pallas_call(
        functools.partial(prepare_kernel, planes, rows, reach),
        grid=(views, 2),
        in_specs=[SMEM_SPEC] * 4,
        out_specs=[spec(*s) for s in shapes],
        out_shape=[jax.ShapeDtypeStruct((views, 2) + s, BF16) for s in shapes],
        cost_estimate=pl.CostEstimate(flops=20_000_000, bytes_accessed=9_000_000, transcendentals=0),
        name="prepare",
    )(wz, wy, wx, parity)


def z_group(w_ref, own, one, two):
    x = jnp.concatenate([v.reshape(-1, v.shape[-1]) for v in (own, one, two)], axis=0)
    hi, lo = halves(x)
    tall = w_ref.shape[0] // 2
    both = mm(w_ref[...], hi)
    out = both[:tall] + both[tall:] + mm(w_ref[:tall], lo)
    return out.reshape(own.shape)


def edge_z_kernel(w_ref, f_ref, a_ref, b_ref, top_ref, bottom_ref):
    top_ref[...] = z_group(w_ref, f_ref[:, :8, :], a_ref[:, :8, :], b_ref[:, :8, :])
    bottom_ref[...] = z_group(w_ref, f_ref[:, 8:, :], a_ref[:, 8:, :], b_ref[:, 8:, :])


def edge_z(w, f, a, b):
    planes, _, width = f.shape
    out = jax.ShapeDtypeStruct((planes, 8, width), F32)
    return pl.pallas_call(
        edge_z_kernel,
        in_specs=[VMEM_SPEC] * 4,
        out_specs=[VMEM_SPEC] * 2,
        out_shape=[out, out],
        cost_estimate=pl.CostEstimate(flops=200_000_000, bytes_accessed=3_000_000, transcendentals=0),
        name="edge_z",
    )(w, f, a, b)


def x_stage(x_buf, rows):
    hi, lo = halves(rows)
    return mm(hi, x_buf[0]) + mm(lo, x_buf[0]) + mm(hi, x_buf[1])


def y_stage(w, x):
    hi, lo = halves(x)
    tall = w.shape[0] // 2
    both = mm(w, hi)
    return both[:tall] + both[tall:] + mm(w[:tall], lo)


def finish(divide, reach, par_ref, result, other, f_ref, a_ref, b_ref):
    out = other / result if divide else other * result
    f_ref[...] = out
    if a_ref is None:
        return
    planes = f_ref.shape[0]
    spare = planes - reach
    par = par_ref[0]
    b_ref[...] = f_ref[pl.ds(spare * par, reach)]
    a_ref[...] = f_ref[pl.ds(spare * (1 - par), reach)]


def edge_kernel(divide, pos, flip, reach, par_ref, view_ref, wz_ref, wy_ref, wx_hbm, f_ref, a_ref, b_ref, top_ref, bottom_ref,
                up_ref, down_ref, other_ref, out_ref, oa_ref, ob_ref, m1_ref, m2_ref, x_buf, rows_buf, m_buf, sems):
    copies = [pltpu.make_async_copy(wx_hbm.at[pos, flip], x_buf, sems.at[0])]
    if divide:
        view = view_ref[0]
        copies.append(pltpu.make_async_copy(other_ref.at[view, :, 0:8, :], m_buf.at[:, 0:8, :], sems.at[1]))
        copies.append(pltpu.make_async_copy(other_ref.at[view, :, 24:32, :], m_buf.at[:, 8:16, :], sems.at[2]))
    for copy in copies:
        copy.start()
    m1_ref[...] = z_group(wz_ref, f_ref[:, :8, :], a_ref[:, :8, :], b_ref[:, :8, :])
    m2_ref[...] = z_group(wz_ref, f_ref[:, 8:, :], a_ref[:, 8:, :], b_ref[:, 8:, :])
    planes, half, width = f_ref.shape
    for q in range(0, planes, 4):
        pieces = []
        for z in range(q, q + 4):
            pieces += [r[z] for r in (up_ref, top_ref, m1_ref, m2_ref, bottom_ref, down_ref)]
        rows_buf[half * q:half * q + 64, :] = y_stage(wy_ref[...], jnp.concatenate(pieces, axis=0))
    copies[0].wait()
    result = x_stage(x_buf, rows_buf[...]).reshape(f_ref.shape)
    for copy in copies[1:]:
        copy.wait()
    finish(divide, reach, par_ref, result, m_buf[...] if divide else other_ref[...], out_ref, oa_ref, ob_ref)


def middle_kernel(divide, pos, flip, reach, par_ref, view_ref, wy_ref, wx_hbm, top_ref, m1_ref, m2_ref, bottom_ref,
                  other_ref, out_ref, oa_ref, ob_ref, x_buf, rows_buf, m_buf, sems):
    copies = [pltpu.make_async_copy(wx_hbm.at[pos, flip], x_buf, sems.at[0])]
    if divide:
        view = view_ref[0]
        copies.append(pltpu.make_async_copy(other_ref.at[view, :, 8:24, :], m_buf, sems.at[1]))
    for copy in copies:
        copy.start()
    planes, half, width = out_ref.shape
    for q in range(0, planes, 8):
        pieces = []
        for z in range(q, q + 8):
            pieces += [r[z] for r in (top_ref, m1_ref, m2_ref, bottom_ref)]
        rows_buf[half * q:half * q + 128, :] = y_stage(wy_ref[...], jnp.concatenate(pieces, axis=0))
    copies[0].wait()
    result = x_stage(x_buf, rows_buf[...]).reshape(out_ref.shape)
    for copy in copies[1:]:
        copy.wait()
    finish(divide, reach, par_ref, result, m_buf[...] if divide else other_ref[...], out_ref, oa_ref, ob_ref)


def scratch(planes, width):
    return [
        pltpu.VMEM((2, width, width), BF16),
        pltpu.VMEM((16 * planes, width), F32),
        pltpu.VMEM((planes, 16, width), F32),
        pltpu.SemaphoreType.DMA((3,)),
    ]


def edge_half(divide, pos, flip, reach, parity, view, wz, wy, wx, f, a, b, top, bottom, up, down, other):
    planes, half, width = f.shape
    whole = jax.ShapeDtypeStruct(f.shape, F32)
    part = jax.ShapeDtypeStruct((reach, half, width), F32)
    group = jax.ShapeDtypeStruct((planes, 8, width), F32)
    return pl.pallas_call(
        functools.partial(edge_kernel, divide, pos, flip, reach),
        in_specs=[SMEM_SPEC] * 2 + [VMEM_SPEC] * 2 + [ANY_SPEC] + [VMEM_SPEC] * 7 + [ANY_SPEC if divide else VMEM_SPEC],
        out_specs=[VMEM_SPEC] * 5,
        out_shape=[whole, part, part, group, group],
        scratch_shapes=scratch(planes, width),
        cost_estimate=pl.CostEstimate(flops=1_000_000_000, bytes_accessed=5_000_000, transcendentals=0),
        name="edge_half",
    )(parity, view, wz, wy, wx, f, a, b, top, bottom, up, down, other)


def middle_half(divide, pos, flip, reach, parity, view, wy, wx, top, m1, m2, bottom, other):
    planes, _, width = top.shape
    whole = jax.ShapeDtypeStruct((planes, 16, width), F32)
    part = jax.ShapeDtypeStruct((reach, 16, width), F32)
    return pl.pallas_call(
        functools.partial(middle_kernel, divide, pos, flip, reach),
        in_specs=[SMEM_SPEC] * 2 + [VMEM_SPEC] + [ANY_SPEC] + [VMEM_SPEC] * 4 + [ANY_SPEC if divide else VMEM_SPEC],
        out_specs=[VMEM_SPEC] * 3,
        out_shape=[whole, part, part],
        scratch_shapes=scratch(planes, width),
        cost_estimate=pl.CostEstimate(flops=1_000_000_000, bytes_accessed=5_000_000, transcendentals=0),
        name="middle_half",
    )(parity, view, wy, wx, top, m1, m2, bottom, other)


def pair_exchange(value, axis, odd):
    size = lax.axis_size(axis)
    pairs = [(i, i + 1) for i in range(odd, size - 1, 2)]
    return lax.ppermute(value, axis, pairs + [(j, i) for i, j in pairs])


def on_device(estimate, measured, psf_z, psf_y, psf_x, extents, order):
    planes, rows, width = estimate.shape
    reach = min(REACH_Z, planes)
    views = measured.shape[0]
    parity_scalar = lax.axis_index("gz") % 2
    parity = jnp.reshape(parity_scalar, (1,)).astype(jnp.int32)
    radii = (extents[order] - 1) // 2
    wz = line_taps(psf_z[order], radii[:, 0], REACH_Z)
    wy = line_taps(psf_y[order], radii[:, 1], REACH_L)
    wx = line_taps(psf_x[order], radii[:, 2], REACH_L)
    mz, mye, mym, mx = prepare(wz, wy, wx, parity, planes, rows, width, reach)

    edge = jnp.concatenate([estimate[:, :8], estimate[:, 24:]], axis=1)
    middle = estimate[:, 8:24]

    def parts(f):
        spare = planes - reach
        a = lax.dynamic_slice_in_dim(f, spare * (1 - parity_scalar), reach, axis=0)
        b = lax.dynamic_slice_in_dim(f, spare * parity_scalar, reach, axis=0)
        return f, a, b

    size_y = lax.axis_size("gy")
    up_pairs = [(i, i + 1) for i in range(size_y - 1)]
    down_pairs = [(j, i) for i, j in up_pairs]

    def blur(divide, pos, flip, view, e, m, other_e, other_m):
        be = pair_exchange(e[2], "gz", 1)
        ae = pair_exchange(e[1], "gz", 0)
        bm = pair_exchange(m[2], "gz", 1)
        am = pair_exchange(m[1], "gz", 0)
        top, bottom = edge_z(mz[pos, flip], e[0], ae, be)
        up = lax.ppermute(bottom, "gy", up_pairs)
        down = lax.ppermute(top, "gy", down_pairs)
        new_e = edge_half(divide, pos, flip, reach, parity, view, mz[pos, flip], mye[pos, flip], mx, m[0], am, bm,
                          top, bottom, up, down, other_e)
        m1, m2 = new_e[3:]
        new_m = middle_half(divide, pos, flip, reach, parity, view, mym[pos, flip], mx, top, m1, m2, bottom, other_m)
        return new_e[:3], new_m

    e, m = parts(edge), parts(middle)
    for pos in range(views):
        view = order[pos:pos + 1]
        re, rm = blur(True, pos, 0, view, e, m, measured, measured)
        e, m = blur(False, pos, 1, view, re, rm, e[0], m[0])
    return jnp.concatenate([e[0][:, :8], m[0], e[0][:, 8:]], axis=1)


def solution(mesh):
    return jax.shard_map(
        on_device,
        mesh=mesh,
        in_specs=(P("gz", "gy", None), P(None, "gz", "gy", None), P(), P(), P(), P(), P()),
        out_specs=P("gz", "gy", None),
        check_vma=False,
    )
```

```python
import functools

import jax
import jax.numpy as jnp
from jax import lax
from jax.experimental import pallas as pl
from jax.experimental.pallas import tpu as pltpu
from jax.sharding import PartitionSpec as P

REACH_Z = 15
REACH_L = 7
TAPS_Z = 2 * REACH_Z + 1
TAPS_L = 2 * REACH_L + 1
F32 = jnp.float32
BF16 = jnp.bfloat16

VMEM_SPEC = pl.BlockSpec(memory_space=pltpu.VMEM)
SMEM_SPEC = pl.BlockSpec(memory_space=pltpu.SMEM)
ANY_SPEC = pl.BlockSpec(memory_space=pl.ANY)


def params(mib):
    return pltpu.CompilerParams(vmem_limit_bytes=mib << 20)


def cost(flops, moved):
    return pl.CostEstimate(flops=flops, bytes_accessed=moved, transcendentals=0)


def halves(x):
    hi = x.astype(BF16)
    return hi, (x - hi.astype(F32)).astype(BF16)


def mm(a, b):
    return jnp.dot(a, b, preferred_element_type=F32)


def stacked(w, x):
    hi, lo = halves(x)
    tall = w.shape[0] // 2
    both = mm(w, hi)
    return both[:tall] + both[tall:] + mm(w[:tall], lo)


def iota2(shape, dim):
    return lax.broadcasted_iota(jnp.int32, shape, dim)


def tap_table(psf_ref, extents_ref, order_ref, pos, flip, axis, count):
    view = order_ref[pos]
    radius = (extents_ref[view, axis] - 1) // 2
    reach = count // 2
    kept = []
    for k in range(count):
        source = jnp.where(flip == 1, count - 1 - k, k)
        kept.append(jnp.where(abs(k - reach) <= radius, psf_ref[view, source], 0.0))
    total = kept[0]
    for tap in kept[1:]:
        total = total + tap
    return kept, total


def banded(place, table):
    kept, total = table
    value = jnp.zeros(place.shape, F32)
    for k, tap in enumerate(kept):
        value = jnp.where(place == k, tap, value)
    return halves(value / jnp.full(place.shape, total, F32))


def prepare_y_kernel(order_ref, extents_ref, psf_ref, par_ref, ye_ref, ym_ref):
    odd = par_ref[1]

    def one(index, carry):
        pos, flip = index // 2, index % 2
        table = tap_table(psf_ref, extents_ref, order_ref, pos, flip, 1, TAPS_L)
        first = jnp.where(odd == 1, 0, 24)
        last = 24 - first
        outer_first = jnp.where(odd == 1, -8, 32)
        outer_last = 24 - outer_first
        r = iota2((64, 192), 0)
        c = iota2((64, 192), 1)
        zc = jnp.where(c >= 144, 3, jnp.where(c >= 96, 2, jnp.where(c >= 48, 1, 0)))
        q = c - 48 * zc
        e = r & 15
        yo = jnp.where(e < 8, e + first, e - 8 + last)
        yi = jnp.where(
            q < 8,
            q + outer_first,
            jnp.where(q < 16, q - 8 + first, jnp.where(q < 32, q - 8, jnp.where(q < 40, q - 32 + last, q - 40 + outer_last))),
        )
        hi, lo = banded(jnp.where((r >> 4) == zc, yi - yo + REACH_L, -1), table)
        ye_ref[pos, flip, :64, :] = hi
        ye_ref[pos, flip, 64:, :] = lo
        r = iota2((128, 256), 0)
        c = iota2((128, 256), 1)
        q = c & 31
        yi = jnp.where(q < 8, q + first, jnp.where(q < 24, q, q - 24 + last))
        hi, lo = banded(jnp.where((r >> 4) == (c >> 5), yi - ((r & 15) + 8) + REACH_L, -1), table)
        ym_ref[pos, flip, :128, :] = hi
        ym_ref[pos, flip, 128:, :] = lo
        return carry

    lax.fori_loop(0, 2 * order_ref.shape[0], one, 0)


def prepare_y(order, extents, psf, parity):
    views = psf.shape[0]
    return pl.pallas_call(
        prepare_y_kernel,
        in_specs=[SMEM_SPEC] * 4,
        out_specs=[VMEM_SPEC] * 2,
        out_shape=[jax.ShapeDtypeStruct((views, 2) + s, BF16) for s in ((128, 192), (256, 256))],
        compiler_params=params(8),
        cost_estimate=cost(5_000_000, 1_000_000),
        name="prepare_y",
    )(order, extents, psf, parity)


def prepare_zx_kernel(planes, order_ref, extents_ref, psf_z_ref, psf_x_ref, par_ref, z_ref, x_ref):
    par = par_ref[0]
    tall = 8 * planes
    wide = z_ref.shape[-1]
    blocks = x_ref.shape[-1] // 128

    def one(index, carry):
        pos, flip = index // 2, index % 2
        table = tap_table(psf_z_ref, extents_ref, order_ref, pos, flip, 0, TAPS_Z)

        def z_rows(chunk, inner):
            base = pl.multiple_of(chunk * 16, 16)
            r = iota2((16, wide), 0) + base
            c = iota2((16, wide), 1)
            plane = c >> 3
            second = plane >= 2 * planes
            j = jnp.where(second, plane - 2 * planes, plane - planes)
            below = jnp.where(second, 1 - par, par) == 1
            i = jnp.where(plane < planes, plane, jnp.where(below, -1 - j, planes + j))
            d = jnp.where((r & 7) == (c & 7), i - (r >> 3) + REACH_Z, -1)
            hi, lo = banded(d, table)
            z_ref[pos, flip, pl.ds(base, 16), :] = hi
            z_ref[pos, flip, pl.ds(tall + base, 16), :] = lo
            return inner

        lax.fori_loop(0, tall // 16, z_rows, 0)

        table_x = tap_table(psf_x_ref, extents_ref, order_ref, pos, flip, 2, TAPS_L)
        d = iota2((128, 128), 0) - iota2((128, 128), 1) + REACH_L
        for shift in (-1, 0, 1):
            hi, lo = banded(d + 128 * shift, table_x)
            for b in range(blocks):
                a = b + shift
                if 0 <= a < blocks:
                    x_ref[pos, flip, 0, 128 * a:128 * a + 128, 128 * b:128 * b + 128] = hi
                    x_ref[pos, flip, 1, 128 * a:128 * a + 128, 128 * b:128 * b + 128] = lo
        zero = jnp.zeros((128, 128), BF16)
        for a in range(blocks):
            for b in range(blocks):
                if abs(a - b) > 1:
                    x_ref[pos, flip, 0, 128 * a:128 * a + 128, 128 * b:128 * b + 128] = zero
                    x_ref[pos, flip, 1, 128 * a:128 * a + 128, 128 * b:128 * b + 128] = zero
        return carry

    lax.fori_loop(0, 2 * order_ref.shape[0], one, 0)


def prepare_zx(order, extents, psf_z, psf_x, parity, planes, width):
    views = psf_z.shape[0]
    shapes = ((16 * planes, 24 * planes), (2, width, width))
    return pl.pallas_call(
        functools.partial(prepare_zx_kernel, planes),
        in_specs=[SMEM_SPEC] * 5,
        out_specs=[VMEM_SPEC] * 2,
        out_shape=[jax.ShapeDtypeStruct((views, 2) + s, BF16) for s in shapes],
        compiler_params=params(8),
        cost_estimate=cost(20_000_000, 10_000_000),
        name="prepare_zx",
    )(order, extents, psf_z, psf_x, parity)


def z_group(w, own, one, two):
    rows = []
    for v in (own, one, two):
        rows.append(v.reshape(-1, v.shape[-1]))
        missing = 8 * (own.shape[0] - v.shape[0])
        if missing:
            rows.append(jnp.zeros((missing, v.shape[-1]), F32))
    return stacked(w, jnp.concatenate(rows, axis=0)).reshape(own.shape)


def x_stage(w, rows):
    hi, lo = halves(rows)
    return mm(hi, w[0]) + mm(lo, w[0]) + mm(hi, w[1])


def zx_stage(wz, wx, own_ref, a_ref, b_ref, z_buf):
    z_buf[:, :8, :] = z_group(wz, own_ref[:, :8, :], a_ref[:, :8, :], b_ref[:, :8, :])
    z_buf[:, 8:, :] = z_group(wz, own_ref[:, 8:, :], a_ref[:, 8:, :], b_ref[:, 8:, :])
    planes, half, width = z_buf.shape
    return x_stage(wx, z_buf[...].reshape(planes * half, width)).reshape(z_buf.shape)


def send_parts(par, whole_ref, a_ref, b_ref):
    last = whole_ref.shape[0] - 1
    for j in range(a_ref.shape[0]):
        b_ref[j] = whole_ref[jnp.where(par == 1, last - j, j)]
        a_ref[j] = whole_ref[jnp.where(par == 1, j, last - j)]


def y_middle(w, e0_ref, m_ref, e1_ref, out_ref):
    for q in range(0, m_ref.shape[0], 8):
        pieces = []
        for z in range(q, q + 8):
            pieces += [r[z] for r in (e0_ref, m_ref, e1_ref)]
        out_ref[q:q + 8] = stacked(w, jnp.concatenate(pieces, axis=0)).reshape(8, 16, m_ref.shape[-1])


def edge_rows(odd):
    first = pl.multiple_of(jnp.where(odd == 1, 0, 24), 8)
    last = pl.multiple_of(jnp.where(odd == 1, 24, 0), 8)
    return pl.ds(first, 8), pl.ds(last, 8)


def start_kernel(par_ref, f_hbm, ym_ref, e0_ref, e1_ref, m_ref, ny_ref, na_ref, nb_ref, sems):
    first, last = edge_rows(par_ref[1])
    copies = [
        pltpu.make_async_copy(f_hbm.at[:, rows, :], out, sems.at[i])
        for i, (rows, out) in enumerate(((first, e0_ref), (last, e1_ref), (pl.ds(8, 16), m_ref)))
    ]
    for copy in copies:
        copy.start()
    for copy in copies:
        copy.wait()
    y_middle(ym_ref[0, 0], e0_ref, m_ref, e1_ref, ny_ref)
    send_parts(par_ref[0], ny_ref, na_ref, nb_ref)


def edge_y_kernel(pos, flip, par_ref, ye_ref, e0_ref, m_ref, e1_ref, r0_ref, r1_ref, ny_ref, na_ref, nb_ref):
    for q in range(0, m_ref.shape[0], 4):
        pieces = []
        for z in range(q, q + 4):
            pieces += [r[z] for r in (r0_ref, e0_ref, m_ref, e1_ref, r1_ref)]
        ny_ref[q:q + 4] = stacked(ye_ref[pos, flip], jnp.concatenate(pieces, axis=0)).reshape(4, 16, m_ref.shape[-1])
    send_parts(par_ref[0], ny_ref, na_ref, nb_ref)


def middle_kernel(pos, flip, view_ref, wz_ref, wx_ref, own_ref, a_ref, b_ref, other_ref, m_ref, z_buf, m_buf, sem):
    if flip == 0:
        copy = pltpu.make_async_copy(other_ref.at[view_ref[pos], :, 8:24, :], m_buf, sem.at[0])
        copy.start()
    result = zx_stage(wz_ref[pos, flip], wx_ref.at[pos, flip], own_ref, a_ref, b_ref, z_buf)
    if flip == 0:
        copy.wait()
        m_ref[...] = m_buf[...] / result
    else:
        m_ref[...] = other_ref[...] * result


def edge_kernel(pos, flip, follows, *refs):
    par_ref, view_ref, wz_ref, wx_ref, ym_ref, own_ref, a_ref, b_ref, m_ref = refs[:9]
    if flip == 0:
        measured_ref = refs[9]
        rest = refs[10:]
    else:
        other0_ref, other1_ref = refs[9:11]
        rest = refs[11:]
    z_buf, m_buf, sems = rest[-3:]
    first, last = edge_rows(par_ref[1])
    if flip == 0:
        view = view_ref[pos]
        copies = [
            pltpu.make_async_copy(measured_ref.at[view, :, rows, :], m_buf.at[:, 8 * i:8 * i + 8, :], sems.at[i])
            for i, rows in enumerate((first, last))
        ]
        for copy in copies:
            copy.start()
    result = zx_stage(wz_ref[pos, flip], wx_ref.at[pos, flip], own_ref, a_ref, b_ref, z_buf)
    if flip == 0:
        for copy in copies:
            copy.wait()
        new0 = m_buf[:, :8, :] / result[:, :8]
        new1 = m_buf[:, 8:, :] / result[:, 8:]
    else:
        new0 = other0_ref[...] * result[:, :8]
        new1 = other1_ref[...] * result[:, 8:]
    if follows is None:
        out_ref = rest[0]
        out_ref[:, first, :] = new0
        out_ref[:, last, :] = new1
        out_ref[:, 8:24, :] = m_ref[...]
    else:
        e0_ref, e1_ref, ny_ref, na_ref, nb_ref = rest[:5]
        e0_ref[...] = new0
        e1_ref[...] = new1
        y_middle(ym_ref[follows[0], follows[1]], e0_ref, m_ref, e1_ref, ny_ref)
        send_parts(par_ref[0], ny_ref, na_ref, nb_ref)


def pair_exchange(value, axis, odd):
    size = lax.axis_size(axis)
    pairs = [(i, i + 1) for i in range(odd, size - 1, 2)]
    return lax.ppermute(value, axis, pairs + [(j, i) for i, j in pairs])


def on_device(estimate, measured, psf_z, psf_y, psf_x, extents, order):
    planes, rows, width = estimate.shape
    reach = min(REACH_Z, planes)
    views = measured.shape[0]
    parity = jnp.stack([lax.axis_index("gz") % 2, lax.axis_index("gy") % 2]).astype(jnp.int32)
    half = jax.ShapeDtypeStruct((planes, 16, width), F32)
    group = jax.ShapeDtypeStruct((planes, 8, width), F32)
    part = jax.ShapeDtypeStruct((reach, 16, width), F32)
    whole = jax.ShapeDtypeStruct(estimate.shape, F32)
    dma = pltpu.SemaphoreType.DMA
    buffers = [pltpu.VMEM(half.shape, F32), pltpu.VMEM(half.shape, F32), dma((2,))]

    mye, mym = prepare_y(order, extents, psf_y, parity)
    e0, e1, m, ny, na, nb = pl.pallas_call(
        start_kernel,
        in_specs=[SMEM_SPEC, ANY_SPEC, VMEM_SPEC],
        out_specs=[VMEM_SPEC] * 6,
        out_shape=[group, group, half, half, part, part],
        scratch_shapes=[dma((3,))],
        compiler_params=params(10),
        cost_estimate=cost(200_000_000, 4_000_000),
        name="start",
    )(parity, estimate, mym)
    mz, mx = prepare_zx(order, extents, psf_z, psf_x, parity, planes, width)

    current = None
    for pos in range(views):
        for flip in (0, 1):
            if flip == 0:
                current = (e0, e1, m)
            bm = pair_exchange(nb, "gz", 1)
            am = pair_exchange(na, "gz", 0)
            r0 = pair_exchange(e0, "gy", 0)
            r1 = pair_exchange(e1, "gy", 1)
            ey, ea, eb = pl.pallas_call(
                functools.partial(edge_y_kernel, pos, flip),
                in_specs=[SMEM_SPEC] + [VMEM_SPEC] * 6,
                out_specs=[VMEM_SPEC] * 3,
                out_shape=[half, part, part],
                compiler_params=params(10),
                cost_estimate=cost(400_000_000, 4_000_000),
                name="edge_y",
            )(parity, mye, e0, m, e1, r0, r1)
            be = pair_exchange(eb, "gz", 1)
            ae = pair_exchange(ea, "gz", 0)
            m_other = [measured] if flip == 0 else [current[2]]
            new_m = pl.pallas_call(
                functools.partial(middle_kernel, pos, flip),
                in_specs=[SMEM_SPEC] + [VMEM_SPEC] * 5 + [ANY_SPEC if flip == 0 else VMEM_SPEC],
                out_specs=VMEM_SPEC,
                out_shape=half,
                scratch_shapes=buffers,
                compiler_params=params(12),
                cost_estimate=cost(1_000_000_000, 4_000_000),
                name="middle",
            )(order, mz, mx, ny, am, bm, *m_other)
            final = pos == views - 1 and flip == 1
            follows = None if final else (pos + flip, 1 - flip)
            e_other = [measured] if flip == 0 else list(current[:2])
            out = pl.pallas_call(
                functools.partial(edge_kernel, pos, flip, follows),
                in_specs=[SMEM_SPEC] * 2 + [VMEM_SPEC] * 7 + ([ANY_SPEC] if flip == 0 else [VMEM_SPEC] * 2),
                out_specs=[VMEM_SPEC] * (1 if final else 5),
                out_shape=[whole] if final else [group, group, half, part, part],
                scratch_shapes=buffers,
                compiler_params=params(12),
                cost_estimate=cost(1_200_000_000, 5_000_000),
                name="edge",
            )(parity, order, mz, mx, mym, ey, ae, be, new_m, *e_other)
            if final:
                return out[0]
            e0, e1, ny, na, nb = out
            m = new_m


def solution(mesh):
    return jax.shard_map(
        on_device,
        mesh=mesh,
        in_specs=(P("gz", "gy", None), P(None, "gz", "gy", None), P(), P(), P(), P(), P()),
        out_specs=P("gz", "gy", None),
        check_vma=False,
    )
```

```python
import functools

import jax
import jax.numpy as jnp
from jax import lax
from jax.experimental import pallas as pl
from jax.experimental.pallas import tpu as pltpu
from jax.sharding import PartitionSpec as P


REACH_Z = 15
REACH_L = 7
TAPS_Z = 2 * REACH_Z + 1
TAPS_L = 2 * REACH_L + 1
REACHES = (7, 11, 15)
F32 = jnp.float32
BF16 = jnp.bfloat16

VMEM_SPEC = pl.BlockSpec(memory_space=pltpu.VMEM)
SMEM_SPEC = pl.BlockSpec(memory_space=pltpu.SMEM)
ANY_SPEC = pl.BlockSpec(memory_space=pl.ANY)


def params(mib):
    return pltpu.CompilerParams(vmem_limit_bytes=mib << 20)


def cost(flops, moved):
    return pl.CostEstimate(flops=flops, bytes_accessed=moved, transcendentals=0)


def halves(x):
    hi = x.astype(BF16)
    return hi, (x - hi.astype(F32)).astype(BF16)


def mm(a, b):
    return jnp.dot(a, b, preferred_element_type=F32)


def stacked(w, x):
    hi, lo = halves(x)
    tall = w.shape[0] // 2
    both = mm(w, hi)
    return both[:tall] + both[tall:] + mm(w[:tall], lo)


def iota2(shape, dim):
    return lax.broadcasted_iota(jnp.int32, shape, dim)


def tap_table(psf_ref, extents_ref, order_ref, pos, flip, axis, count):
    view = order_ref[pos]
    radius = (extents_ref[view, axis] - 1) // 2
    reach = count // 2
    kept = []
    for k in range(count):
        source = jnp.where(flip == 1, count - 1 - k, k)
        kept.append(jnp.where(abs(k - reach) <= radius, psf_ref[view, source], 0.0))
    total = kept[0]
    for tap in kept[1:]:
        total = total + tap
    return kept, total


def banded(place, table):
    kept, total = table
    value = jnp.zeros(place.shape, F32)
    for k, tap in enumerate(kept):
        value = jnp.where(place == k, tap, value)
    return halves(value / jnp.full(place.shape, total, F32))


def middle_bands(table, odd):
    first = jnp.where(odd == 1, 0, 24)
    last = 24 - first
    r = iota2((128, 256), 0)
    c = iota2((128, 256), 1)
    q = c & 31
    yi = jnp.where(q < 8, q + first, jnp.where(q < 24, q, q - 24 + last))
    return banded(jnp.where((r >> 4) == (c >> 5), yi - ((r & 15) + 8) + REACH_L, -1), table)


def edge_bands(table, odd):
    first = jnp.where(odd == 1, 0, 24)
    last = 24 - first
    outer_first = jnp.where(odd == 1, -8, 32)
    outer_last = 24 - outer_first
    r = iota2((64, 192), 0)
    c = iota2((64, 192), 1)
    zc = jnp.where(c >= 144, 3, jnp.where(c >= 96, 2, jnp.where(c >= 48, 1, 0)))
    q = c - 48 * zc
    e = r & 15
    yo = jnp.where(e < 8, e + first, e - 8 + last)
    yi = jnp.where(
        q < 8,
        q + outer_first,
        jnp.where(q < 16, q - 8 + first, jnp.where(q < 32, q - 8, jnp.where(q < 40, q - 32 + last, q - 40 + outer_last))),
    )
    return banded(jnp.where((r >> 4) == zc, yi - yo + REACH_L, -1), table)


def prepare_kernel(planes, pos_ref, order_ref, extents_ref, psf_z_ref, psf_y_ref, psf_x_ref, par_ref, ye_ref, ym_ref, z_ref, x_ref):
    par = par_ref[0]
    pos = pos_ref[0]
    tall = 8 * planes
    wide = z_ref.shape[-1]
    blocks = x_ref.shape[-1] // 128

    def one(flip, carry):
        table = tap_table(psf_y_ref, extents_ref, order_ref, pos, flip, 1, TAPS_L)
        hi, lo = edge_bands(table, par_ref[1])
        ye_ref[flip, :64, :] = hi
        ye_ref[flip, 64:, :] = lo
        hi, lo = middle_bands(table, par_ref[1])
        ym_ref[flip, :128, :] = hi
        ym_ref[flip, 128:, :] = lo

        table = tap_table(psf_z_ref, extents_ref, order_ref, pos, flip, 0, TAPS_Z)

        def z_rows(chunk, inner):
            base = pl.multiple_of(chunk * 16, 16)
            r = iota2((16, wide), 0) + base
            c = iota2((16, wide), 1)
            plane = c >> 3
            second = plane >= 2 * planes
            j = jnp.where(second, plane - 2 * planes, plane - planes)
            below = jnp.where(second, 1 - par, par) == 1
            i = jnp.where(plane < planes, plane, jnp.where(below, -1 - j, planes + j))
            d = jnp.where((r & 7) == (c & 7), i - (r >> 3) + REACH_Z, -1)
            hi, lo = banded(d, table)
            z_ref[flip, pl.ds(base, 16), :] = hi
            z_ref[flip, pl.ds(tall + base, 16), :] = lo
            return inner

        lax.fori_loop(0, tall // 16, z_rows, 0)

        table = tap_table(psf_x_ref, extents_ref, order_ref, pos, flip, 2, TAPS_L)
        d = iota2((128, 128), 0) - iota2((128, 128), 1) + REACH_L
        for shift in (-1, 0, 1):
            hi, lo = banded(d + 128 * shift, table)
            for b in range(blocks):
                a = b + shift
                if 0 <= a < blocks:
                    x_ref[flip, 0, 128 * a:128 * a + 128, 128 * b:128 * b + 128] = hi
                    x_ref[flip, 1, 128 * a:128 * a + 128, 128 * b:128 * b + 128] = lo
        zero = jnp.zeros((128, 128), BF16)
        for a in range(blocks):
            for b in range(blocks):
                if abs(a - b) > 1:
                    x_ref[flip, 0, 128 * a:128 * a + 128, 128 * b:128 * b + 128] = zero
                    x_ref[flip, 1, 128 * a:128 * a + 128, 128 * b:128 * b + 128] = zero
        return carry

    lax.fori_loop(0, 2, one, 0)


def tall_rows(planes, *values):
    rows = []
    for v in values:
        rows.append(v.reshape(-1, v.shape[-1]))
        missing = 8 * (planes - v.shape[0])
        if missing:
            rows.append(jnp.zeros((missing, v.shape[-1]), F32))
    return jnp.concatenate(rows, axis=0)


def x_stage(w, rows):
    hi, lo = halves(rows)
    return mm(hi, w[0]) + mm(lo, w[0]) + mm(hi, w[1])


def inner_z(wz, own_ref, a_ref, out_ref):
    planes, half, width = out_ref.shape
    split = 16 * planes
    for g in range(0, half, 8):
        x = tall_rows(planes, own_ref[:, g:g + 8, :], a_ref[:, g:g + 8, :])
        out_ref[:, g:g + 8, :] = stacked(wz[:, :split], x).reshape(planes, 8, width)


def outer_zx(wz, wx, inner_ref, b_ref, z_buf):
    planes, half, width = z_buf.shape
    split = 16 * planes
    for g in range(0, half, 8):
        x = tall_rows(planes, b_ref[:, g:g + 8, :])
        z_buf[:, g:g + 8, :] = inner_ref[:, g:g + 8, :] + stacked(wz[:, split:], x).reshape(planes, 8, width)
    return x_stage(wx, z_buf[...].reshape(planes * half, width)).reshape(z_buf.shape)


def zx_stage(wz, wx, own_ref, a_ref, b_ref, z_buf):
    planes, half, width = z_buf.shape
    for g in range(0, half, 8):
        x = tall_rows(planes, own_ref[:, g:g + 8, :], a_ref[:, g:g + 8, :], b_ref[:, g:g + 8, :])
        z_buf[:, g:g + 8, :] = stacked(wz, x).reshape(planes, 8, width)
    return x_stage(wx, z_buf[...].reshape(planes * half, width)).reshape(z_buf.shape)


def send_parts(par, whole_ref, a_ref, b_ref):
    last = whole_ref.shape[0] - 1

    def one(j, carry):
        b_ref[j] = whole_ref[jnp.where(par == 1, last - j, j)]
        a_ref[j] = whole_ref[jnp.where(par == 1, j, last - j)]
        return carry

    lax.fori_loop(0, a_ref.shape[0], one, 0)


def y_middle(w, e0_ref, m_ref, e1_ref, out_ref):
    for q in range(0, m_ref.shape[0], 8):
        pieces = []
        for z in range(q, q + 8):
            pieces += [r[z] for r in (e0_ref, m_ref, e1_ref)]
        out_ref[q:q + 8] = stacked(w, jnp.concatenate(pieces, axis=0)).reshape(8, 16, m_ref.shape[-1])


def edge_rows(odd):
    first = pl.multiple_of(jnp.where(odd == 1, 0, 24), 8)
    last = pl.multiple_of(jnp.where(odd == 1, 24, 0), 8)
    return pl.ds(first, 8), pl.ds(last, 8)


def split_kernel(par_ref, f_hbm, e0_ref, e1_ref, m_ref, sems):
    first, last = edge_rows(par_ref[1])
    copies = [
        pltpu.make_async_copy(f_hbm.at[:, rows, :], out, sems.at[i])
        for i, (rows, out) in enumerate(((first, e0_ref), (last, e1_ref), (pl.ds(8, 16), m_ref)))
    ]
    for copy in copies:
        copy.start()
    for copy in copies:
        copy.wait()


def merge_kernel(par_ref, e0_ref, e1_ref, m_ref, out_ref):
    first, last = edge_rows(par_ref[1])
    out_ref[:, first, :] = e0_ref[...]
    out_ref[:, last, :] = e1_ref[...]
    out_ref[:, 8:24, :] = m_ref[...]


def open_kernel(pos_ref, order_ref, extents_ref, psf_ref, par_ref, e0_ref, m_ref, e1_ref, ny_ref, na_ref, nb_ref, w_buf):
    hi, lo = middle_bands(tap_table(psf_ref, extents_ref, order_ref, pos_ref[0], 0, 1, TAPS_L), par_ref[1])
    w_buf[:128, :] = hi
    w_buf[128:, :] = lo
    y_middle(w_buf[...], e0_ref, m_ref, e1_ref, ny_ref)
    send_parts(par_ref[0], ny_ref, na_ref, nb_ref)


def edge_y_kernel(flip, par_ref, ye_ref, e0_ref, m_ref, e1_ref, r0_ref, r1_ref, ny_ref, na_ref, nb_ref):
    for q in range(0, m_ref.shape[0], 4):
        pieces = []
        for z in range(q, q + 4):
            pieces += [r[z] for r in (r0_ref, e0_ref, m_ref, e1_ref, r1_ref)]
        ny_ref[q:q + 4] = stacked(ye_ref[flip], jnp.concatenate(pieces, axis=0)).reshape(4, 16, m_ref.shape[-1])
    send_parts(par_ref[0], ny_ref, na_ref, nb_ref)


def inner_kernel(flip, wz_ref, own_ref, a_ref, out_ref):
    inner_z(wz_ref[flip], own_ref, a_ref, out_ref)


def middle_kernel(flip, pos_ref, order_ref, wz_ref, wx_ref, own_ref, a_ref, b_ref, other_ref, m_ref, z_buf, m_buf, sem):
    if flip == 0:
        copy = pltpu.make_async_copy(other_ref.at[order_ref[pos_ref[0]], :, 8:24, :], m_buf, sem.at[0])
        copy.start()
    result = zx_stage(wz_ref[flip], wx_ref.at[flip], own_ref, a_ref, b_ref, z_buf)
    if flip == 0:
        copy.wait()
        m_ref[...] = m_buf[...] / result
    else:
        m_ref[...] = other_ref[...] * result


def forward_edge_kernel(par_ref, pos_ref, order_ref, wz_ref, wx_ref, ym_ref, inner_ref, b_ref, m_ref, measured_ref,
                        e0_ref, e1_ref, ny_ref, na_ref, nb_ref, z_buf, m_buf, sems):
    first, last = edge_rows(par_ref[1])
    view = order_ref[pos_ref[0]]
    copies = [
        pltpu.make_async_copy(measured_ref.at[view, :, rows, :], m_buf.at[:, 8 * i:8 * i + 8, :], sems.at[i])
        for i, rows in enumerate((first, last))
    ]
    for copy in copies:
        copy.start()
    result = outer_zx(wz_ref[0], wx_ref.at[0], inner_ref, b_ref, z_buf)
    for copy in copies:
        copy.wait()
    e0_ref[...] = m_buf[:, :8, :] / result[:, :8]
    e1_ref[...] = m_buf[:, 8:, :] / result[:, 8:]
    y_middle(ym_ref[1], e0_ref, m_ref, e1_ref, ny_ref)
    send_parts(par_ref[0], ny_ref, na_ref, nb_ref)


def adjoint_edge_kernel(wz_ref, wx_ref, inner_ref, b_ref, other0_ref, other1_ref, e0_ref, e1_ref, z_buf):
    result = outer_zx(wz_ref[1], wx_ref.at[1], inner_ref, b_ref, z_buf)
    e0_ref[...] = other0_ref[...] * result[:, :8]
    e1_ref[...] = other1_ref[...] * result[:, 8:]


def pair_exchange(value, axis, odd):
    size = lax.axis_size(axis)
    pairs = [(i, i + 1) for i in range(odd, size - 1, 2)]
    return lax.ppermute(value, axis, pairs + [(j, i) for i, j in pairs])


def call(kernel, ins, outs, flops, scratch=(), mib=12):
    return pl.pallas_call(
        kernel,
        in_specs=ins,
        out_specs=[VMEM_SPEC] * len(outs),
        out_shape=outs,
        scratch_shapes=list(scratch),
        compiler_params=params(mib),
        cost_estimate=cost(flops, 4_000_000),
    )


def view_pass(reach, shapes, parity, tables, measured, pos, e0, e1, m):
    group, half = shapes
    planes, _, width = half.shape
    order, extents, psf_z, psf_y, psf_x = tables
    part = jax.ShapeDtypeStruct((reach, 16, width), F32)
    dma = pltpu.SemaphoreType.DMA
    z_buf = pltpu.VMEM(half.shape, F32)
    m_buf = pltpu.VMEM(half.shape, F32)
    sm, vm = SMEM_SPEC, VMEM_SPEC

    ny, na, nb = call(open_kernel, [sm] * 5 + [vm] * 3, [half, part, part], 200_000_000,
                      [pltpu.VMEM((256, 256), BF16)])(pos, order, extents, psf_y, parity, e0, m, e1)
    weights = [jax.ShapeDtypeStruct((2,) + s, BF16)
               for s in ((128, 192), (256, 256), (16 * planes, 24 * planes), (2, width, width))]
    mye, mym, mz, mx = call(functools.partial(prepare_kernel, planes), [sm] * 7, weights, 20_000_000, mib=8)(
        pos, order, extents, psf_z, psf_y, psf_x, parity)
    current = (e0, e1, m)
    for flip in (0, 1):
        r1 = pair_exchange(e1, "gy", 1)
        bm = pair_exchange(nb, "gz", 1)
        r0 = pair_exchange(e0, "gy", 0)
        am = pair_exchange(na, "gz", 0)
        ey, ea, eb = call(functools.partial(edge_y_kernel, flip), [sm] + [vm] * 6, [half, part, part],
                          400_000_000)(parity, mye, e0, m, e1, r0, r1)
        be = pair_exchange(eb, "gz", 1)
        ae = pair_exchange(ea, "gz", 0)
        m, = call(functools.partial(middle_kernel, flip), [sm] * 2 + [vm] * 5 + [vm if flip else ANY_SPEC],
                  [half], 1_000_000_000, [z_buf, m_buf, dma((1,))])(
            pos, order, mz, mx, ny, am, bm, current[2] if flip else measured)
        inner, = call(functools.partial(inner_kernel, flip), [vm] * 3, [half], 400_000_000)(mz, ey, ae)
        if flip == 0:
            e0, e1, ny, na, nb = call(forward_edge_kernel, [sm] * 3 + [vm] * 6 + [ANY_SPEC],
                                      [group, group, half, part, part], 1_200_000_000, [z_buf, m_buf, dma((2,))])(
                parity, pos, order, mz, mx, mym, inner, be, m, measured)
        else:
            e0, e1 = call(adjoint_edge_kernel, [vm] * 6, [group, group], 1_000_000_000, [z_buf])(
                mz, mx, inner, be, current[0], current[1])
    return e0, e1, m


def on_device(estimate, measured, psf_z, psf_y, psf_x, extents, order):
    planes, _, width = estimate.shape
    views = measured.shape[0]
    reaches = tuple(min(r, planes) for r in REACHES)
    parity = jnp.stack([lax.axis_index("gz") & 1, lax.axis_index("gy") & 1]).astype(jnp.int32)
    half = jax.ShapeDtypeStruct((planes, 16, width), F32)
    group = jax.ShapeDtypeStruct((planes, 8, width), F32)
    whole = jax.ShapeDtypeStruct(estimate.shape, F32)
    tables = (order, extents, psf_z, psf_y, psf_x)
    radii = (extents[:, 0] - 1) // 2
    sizes = sum((radii > r).astype(jnp.int32) for r in REACHES[:-1]) if len(REACHES) > 1 else jnp.zeros_like(radii)

    state = call(split_kernel, [SMEM_SPEC, ANY_SPEC], [group, group, half], 1, [pltpu.SemaphoreType.DMA((3,))])(
        parity, estimate)
    passes = [functools.partial(view_pass, r, (group, half), parity, tables, measured) for r in reaches]
    packed = jnp.sum(sizes[order] << (2 * jnp.arange(views, dtype=jnp.int32)))

    def step(index, state):
        pos = jnp.reshape(index, (1,)).astype(jnp.int32)
        if len(passes) == 1:
            return (state[0],) + tuple(passes[0](pos, *state[1:]))
        return (state[0] >> 2,) + tuple(lax.switch(state[0] & 3, passes, pos, *state[1:]))

    state = lax.fori_loop(0, views, step, (packed, *state))[1:]
    return call(merge_kernel, [SMEM_SPEC] + [VMEM_SPEC] * 3, [whole], 1)(parity, *state)[0]


def solution(mesh):
    return jax.shard_map(
        on_device,
        mesh=mesh,
        in_specs=(P("gz", "gy", None), P(None, "gz", "gy", None), P(), P(), P(), P(), P()),
        out_specs=P("gz", "gy", None),
        check_vma=False,
    )
```

```python
import functools

import jax
import jax.numpy as jnp
from jax import lax
from jax.experimental import pallas as pl
from jax.experimental.pallas import tpu as pltpu
from jax.sharding import PartitionSpec as P


REACH_Z = 15
REACH_L = 7
TAPS_Z = 2 * REACH_Z + 1
TAPS_L = 2 * REACH_L + 1
REACHES = (6, 9, 12, 15)
F32 = jnp.float32
BF16 = jnp.bfloat16

VMEM_SPEC = pl.BlockSpec(memory_space=pltpu.VMEM)
SMEM_SPEC = pl.BlockSpec(memory_space=pltpu.SMEM)
ANY_SPEC = pl.BlockSpec(memory_space=pl.ANY)


def params(mib):
    return pltpu.CompilerParams(vmem_limit_bytes=mib << 20)


def cost(flops, moved):
    return pl.CostEstimate(flops=flops, bytes_accessed=moved, transcendentals=0)


def halves(x):
    hi = x.astype(BF16)
    return hi, (x - hi.astype(F32)).astype(BF16)


def mm(a, b):
    return jnp.dot(a, b, preferred_element_type=F32)


def stacked(w, x):
    hi, lo = halves(x)
    tall = w.shape[0] // 2
    both = mm(w, hi)
    return both[:tall] + both[tall:] + mm(w[:tall], lo)


def iota2(shape, dim):
    return lax.broadcasted_iota(jnp.int32, shape, dim)


def tap_table(psf_ref, extents_ref, order_ref, pos, flip, axis, count):
    view = order_ref[pos]
    radius = (extents_ref[view, axis] - 1) // 2
    reach = count // 2
    kept = []
    for k in range(count):
        source = jnp.where(flip == 1, count - 1 - k, k)
        kept.append(jnp.where(abs(k - reach) <= radius, psf_ref[view, source], 0.0))
    total = kept[0]
    for tap in kept[1:]:
        total = total + tap
    return kept, total


def banded(place, table):
    kept, total = table
    value = jnp.zeros(place.shape, F32)
    for k, tap in enumerate(kept):
        value = jnp.where(place == k, tap, value)
    return halves(value / jnp.full(place.shape, total, F32))


def middle_bands(table, odd):
    first = jnp.where(odd == 1, 0, 24)
    last = 24 - first
    r = iota2((128, 256), 0)
    c = iota2((128, 256), 1)
    q = c & 31
    yi = jnp.where(q < 8, q + first, jnp.where(q < 24, q, q - 24 + last))
    return banded(jnp.where((r >> 4) == (c >> 5), yi - ((r & 15) + 8) + REACH_L, -1), table)


def edge_bands(table, odd):
    first = jnp.where(odd == 1, 0, 24)
    last = 24 - first
    outer_first = jnp.where(odd == 1, -8, 32)
    outer_last = 24 - outer_first
    r = iota2((64, 192), 0)
    c = iota2((64, 192), 1)
    zc = jnp.where(c >= 144, 3, jnp.where(c >= 96, 2, jnp.where(c >= 48, 1, 0)))
    q = c - 48 * zc
    e = r & 15
    yo = jnp.where(e < 8, e + first, e - 8 + last)
    yi = jnp.where(
        q < 8,
        q + outer_first,
        jnp.where(q < 16, q - 8 + first, jnp.where(q < 32, q - 8, jnp.where(q < 40, q - 32 + last, q - 40 + outer_last))),
    )
    return banded(jnp.where((r >> 4) == zc, yi - yo + REACH_L, -1), table)


def prepare_first_kernel(pos_ref, order_ref, extents_ref, psf_y_ref, par_ref, ye_ref):
    hi, lo = edge_bands(tap_table(psf_y_ref, extents_ref, order_ref, pos_ref[0], 0, 1, TAPS_L), par_ref[1])
    ye_ref[:64, :] = hi
    ye_ref[64:, :] = lo


def prepare_rest_kernel(planes, pos_ref, order_ref, extents_ref, psf_z_ref, psf_y_ref, psf_x_ref, par_ref, after_ref,
                        ye_ref, ym_ref, z_ref, x_ref):
    table = tap_table(psf_y_ref, extents_ref, order_ref, pos_ref[0], 1, 1, TAPS_L)
    hi, lo = edge_bands(table, par_ref[1])
    ye_ref[:64, :] = hi
    ye_ref[64:, :] = lo
    hi, lo = middle_bands(table, par_ref[1])
    ym_ref[:128, :] = hi
    ym_ref[128:, :] = lo
    par = par_ref[0]
    pos = pos_ref[0]
    tall = 8 * planes
    wide = z_ref.shape[-1]
    blocks = x_ref.shape[-1] // 128

    def one(flip, carry):
        table = tap_table(psf_z_ref, extents_ref, order_ref, pos, flip, 0, TAPS_Z)

        def z_rows(chunk, inner):
            base = pl.multiple_of(chunk * 16, 16)
            r = iota2((16, wide), 0) + base
            c = iota2((16, wide), 1)
            plane = c >> 3
            second = plane >= 2 * planes
            j = jnp.where(second, plane - 2 * planes, plane - planes)
            below = jnp.where(second, 1 - par, par) == 1
            i = jnp.where(plane < planes, plane, jnp.where(below, -1 - j, planes + j))
            d = jnp.where((r & 7) == (c & 7), i - (r >> 3) + REACH_Z, -1)
            hi, lo = banded(d, table)
            z_ref[flip, pl.ds(base, 16), :] = hi
            z_ref[flip, pl.ds(tall + base, 16), :] = lo
            return inner

        lax.fori_loop(0, tall // 16, z_rows, 0)

        table = tap_table(psf_x_ref, extents_ref, order_ref, pos, flip, 2, TAPS_L)
        d = iota2((128, 128), 0) - iota2((128, 128), 1) + REACH_L
        for shift in (-1, 0, 1):
            hi, lo = banded(d + 128 * shift, table)
            for b in range(blocks):
                a = b + shift
                if 0 <= a < blocks:
                    x_ref[flip, 0, 128 * a:128 * a + 128, 128 * b:128 * b + 128] = hi
                    x_ref[flip, 1, 128 * a:128 * a + 128, 128 * b:128 * b + 128] = lo
        zero = jnp.zeros((128, 128), BF16)
        for a in range(blocks):
            for b in range(blocks):
                if abs(a - b) > 1:
                    x_ref[flip, 0, 128 * a:128 * a + 128, 128 * b:128 * b + 128] = zero
                    x_ref[flip, 1, 128 * a:128 * a + 128, 128 * b:128 * b + 128] = zero
        return carry

    lax.fori_loop(0, 2, one, 0)


def tall_rows(planes, *values):
    rows = []
    for v in values:
        rows.append(v.reshape(-1, v.shape[-1]))
        missing = 8 * (planes - v.shape[0])
        if missing:
            rows.append(jnp.zeros((missing, v.shape[-1]), F32))
    return jnp.concatenate(rows, axis=0)


def x_stage(w, rows):
    hi, lo = halves(rows)
    return mm(hi, w[0]) + mm(lo, w[0]) + mm(hi, w[1])


def inner_z(wz, own_ref, a_ref, out_ref):
    planes, half, width = out_ref.shape
    split = 16 * planes
    for g in range(0, half, 8):
        x = tall_rows(planes, own_ref[:, g:g + 8, :], a_ref[:, 16 + g:24 + g, :])
        out_ref[:, g:g + 8, :] = stacked(wz[:, :split], x).reshape(planes, 8, width)


def outer_zx(wz, wx, inner_ref, b_ref, z_buf):
    planes, half, width = z_buf.shape
    split = 16 * planes
    for g in range(0, half, 8):
        x = tall_rows(planes, b_ref[:, g:g + 8, :])
        z_buf[:, g:g + 8, :] = inner_ref[:, g:g + 8, :] + stacked(wz[:, split:], x).reshape(planes, 8, width)
    return x_stage(wx, z_buf[...].reshape(planes * half, width)).reshape(z_buf.shape)


def zx_stage(wz, wx, own_ref, a_ref, b_ref, z_buf):
    planes, half, width = z_buf.shape

    def one(group, carry):
        rows = pl.ds(pl.multiple_of(8 * group, 8), 8)
        x = tall_rows(planes, own_ref[:, rows, :], a_ref[:, rows, :], b_ref[:, rows, :])
        z_buf[:, rows, :] = stacked(wz, x).reshape(planes, 8, width)
        return carry

    lax.fori_loop(0, half // 8, one, 0)
    return x_stage(wx, z_buf[...].reshape(planes * half, width)).reshape(z_buf.shape)


def send_outer(par, whole_ref, b_ref):
    last = whole_ref.shape[0] - 1

    def one(j, carry):
        b_ref[j] = whole_ref[jnp.where(par == 1, last - j, j)]
        return carry

    lax.fori_loop(0, b_ref.shape[0], one, 0)


def send_inner(par, middle_ref, edge_ref, a_ref):
    last = middle_ref.shape[0] - 1

    def one(j, carry):
        plane = jnp.where(par == 1, j, last - j)
        a_ref[j, :16, :] = middle_ref[plane]
        a_ref[j, 16:, :] = edge_ref[plane]
        return carry

    lax.fori_loop(0, a_ref.shape[0], one, 0)


def y_middle(w, e0_ref, m_ref, e1_ref, out_ref):
    for q in range(0, m_ref.shape[0], 8):
        pieces = []
        for z in range(q, q + 8):
            pieces += [r[z] for r in (e0_ref, m_ref, e1_ref)]
        out_ref[q:q + 8] = stacked(w, jnp.concatenate(pieces, axis=0)).reshape(8, 16, m_ref.shape[-1])


def edge_rows(odd):
    first = pl.multiple_of(jnp.where(odd == 1, 0, 24), 8)
    last = pl.multiple_of(jnp.where(odd == 1, 24, 0), 8)
    return pl.ds(first, 8), pl.ds(last, 8)


def split_kernel(par_ref, f_hbm, e0_ref, e1_ref, m_ref, sems):
    first, last = edge_rows(par_ref[1])
    copies = [
        pltpu.make_async_copy(f_hbm.at[:, rows, :], out, sems.at[i])
        for i, (rows, out) in enumerate(((first, e0_ref), (last, e1_ref), (pl.ds(8, 16), m_ref)))
    ]
    for copy in copies:
        copy.start()
    for copy in copies:
        copy.wait()


def merge_kernel(par_ref, e0_ref, e1_ref, m_ref, out_ref):
    first, last = edge_rows(par_ref[1])
    out_ref[:, first, :] = e0_ref[...]
    out_ref[:, last, :] = e1_ref[...]
    out_ref[:, 8:24, :] = m_ref[...]


def open_kernel(pos_ref, order_ref, extents_ref, psf_ref, par_ref, e0_ref, m_ref, e1_ref, ny_ref, nb_ref, w_buf):
    hi, lo = middle_bands(tap_table(psf_ref, extents_ref, order_ref, pos_ref[0], 0, 1, TAPS_L), par_ref[1])
    w_buf[:128, :] = hi
    w_buf[128:, :] = lo
    y_middle(w_buf[...], e0_ref, m_ref, e1_ref, ny_ref)
    send_outer(par_ref[0], ny_ref, nb_ref)


def edge_y_kernel(par_ref, ye_ref, e0_ref, m_ref, e1_ref, r0_ref, r1_ref, middle_ref, ny_ref, na_ref, nb_ref):
    for q in range(0, m_ref.shape[0], 4):
        pieces = []
        for z in range(q, q + 4):
            pieces += [r[z] for r in (r0_ref, e0_ref, m_ref, e1_ref, r1_ref)]
        ny_ref[q:q + 4] = stacked(ye_ref[...], jnp.concatenate(pieces, axis=0)).reshape(4, 16, m_ref.shape[-1])
    send_outer(par_ref[0], ny_ref, nb_ref)
    send_inner(par_ref[0], middle_ref, ny_ref, na_ref)


def inner_kernel(flip, wz_ref, own_ref, a_ref, out_ref):
    inner_z(wz_ref[flip], own_ref, a_ref, out_ref)


def middle_kernel(flip, pos_ref, order_ref, wz_ref, wx_ref, own_ref, a_ref, b_ref, other_ref, m_ref, z_buf, m_buf, sem):
    if flip == 0:
        copy = pltpu.make_async_copy(other_ref.at[order_ref[pos_ref[0]], :, 8:24, :], m_buf, sem.at[0])
        copy.start()
    result = zx_stage(wz_ref[flip], wx_ref.at[flip], own_ref, a_ref, b_ref, z_buf)
    if flip == 0:
        copy.wait()
        m_ref[...] = m_buf[...] / result
    else:
        m_ref[...] = other_ref[...] * result


def forward_edge_kernel(par_ref, pos_ref, order_ref, wz_ref, wx_ref, ym_ref, inner_ref, b_ref, m_ref, measured_ref,
                        e0_ref, e1_ref, ny_ref, nb_ref, z_buf, m_buf, sems):
    first, last = edge_rows(par_ref[1])
    view = order_ref[pos_ref[0]]
    copies = [
        pltpu.make_async_copy(measured_ref.at[view, :, rows, :], m_buf.at[:, 8 * i:8 * i + 8, :], sems.at[i])
        for i, rows in enumerate((first, last))
    ]
    for copy in copies:
        copy.start()
    result = outer_zx(wz_ref[0], wx_ref.at[0], inner_ref, b_ref, z_buf)
    for copy in copies:
        copy.wait()
    e0_ref[...] = m_buf[:, :8, :] / result[:, :8]
    e1_ref[...] = m_buf[:, 8:, :] / result[:, 8:]
    y_middle(ym_ref[...], e0_ref, m_ref, e1_ref, ny_ref)
    send_outer(par_ref[0], ny_ref, nb_ref)


def adjoint_edge_kernel(wz_ref, wx_ref, inner_ref, b_ref, other0_ref, other1_ref, e0_ref, e1_ref, z_buf):
    result = outer_zx(wz_ref[1], wx_ref.at[1], inner_ref, b_ref, z_buf)
    e0_ref[...] = other0_ref[...] * result[:, :8]
    e1_ref[...] = other1_ref[...] * result[:, 8:]


def pair_exchange(value, axis, odd):
    size = lax.axis_size(axis)
    pairs = [(i, i + 1) for i in range(odd, size - 1, 2)]
    return lax.ppermute(value, axis, pairs + [(j, i) for i, j in pairs])


def call(kernel, ins, outs, flops, scratch=(), mib=12):
    return pl.pallas_call(
        kernel,
        in_specs=ins,
        out_specs=[VMEM_SPEC] * len(outs),
        out_shape=outs,
        scratch_shapes=list(scratch),
        compiler_params=params(mib),
        cost_estimate=cost(flops, 4_000_000),
    )


def view_pass(reach, shapes, parity, tables, measured, pos, e0, e1, m):
    group, half = shapes
    planes, _, width = half.shape
    order, extents, psf_z, psf_y, psf_x = tables
    part = jax.ShapeDtypeStruct((reach, 16, width), F32)
    both = jax.ShapeDtypeStruct((reach, 32, width), F32)
    dma = pltpu.SemaphoreType.DMA
    z_buf = pltpu.VMEM(half.shape, F32)
    m_buf = pltpu.VMEM(half.shape, F32)
    sm, vm = SMEM_SPEC, VMEM_SPEC

    ny, nb = call(open_kernel, [sm] * 5 + [vm] * 3, [half, part], 200_000_000,
                      [pltpu.VMEM((256, 256), BF16)])(pos, order, extents, psf_y, parity, e0, m, e1)
    wye, wym, wz, wx = [jax.ShapeDtypeStruct(s, BF16)
                        for s in ((128, 192), (256, 256), (2, 16 * planes, 24 * planes), (2, 2, width, width))]
    mye, = call(prepare_first_kernel, [sm] * 5, [wye], 1_000_000, mib=8)(pos, order, extents, psf_y, parity)
    current = (e0, e1, m)
    for flip in (0, 1):
        r1 = pair_exchange(e1, "gy", 1)
        bm = pair_exchange(nb, "gz", 1)
        r0 = pair_exchange(e0, "gy", 0)
        ey, ea, eb = call(edge_y_kernel, [sm] + [vm] * 7, [half, both, part],
                          400_000_000)(parity, mye, e0, m, e1, r0, r1, ny)
        if flip == 0:
            mye, mym, mz, mx = call(functools.partial(prepare_rest_kernel, planes), [sm] * 7 + [ANY_SPEC],
                                    [wye, wym, wz, wx], 20_000_000, mib=8)(
                pos, order, extents, psf_z, psf_y, psf_x, parity, ey)
        be = pair_exchange(eb, "gz", 1)
        ae = pair_exchange(ea, "gz", 0)
        m, = call(functools.partial(middle_kernel, flip), [sm] * 2 + [vm] * 5 + [vm if flip else ANY_SPEC],
                  [half], 1_000_000_000, [z_buf, m_buf, dma((1,))])(
            pos, order, mz, mx, ny, ae, bm, current[2] if flip else measured)
        inner, = call(functools.partial(inner_kernel, flip), [vm] * 3, [half], 400_000_000)(mz, ey, ae)
        if flip == 0:
            e0, e1, ny, nb = call(forward_edge_kernel, [sm] * 3 + [vm] * 6 + [ANY_SPEC],
                                      [group, group, half, part], 1_200_000_000, [z_buf, m_buf, dma((2,))])(
                parity, pos, order, mz, mx, mym, inner, be, m, measured)
        else:
            e0, e1 = call(adjoint_edge_kernel, [vm] * 6, [group, group], 1_000_000_000, [z_buf])(
                mz, mx, inner, be, current[0], current[1])
    return e0, e1, m


def on_device(estimate, measured, psf_z, psf_y, psf_x, extents, order):
    planes, _, width = estimate.shape
    views = measured.shape[0]
    reaches = tuple(min(r, planes) for r in REACHES)
    parity = jnp.stack([lax.axis_index("gz") & 1, lax.axis_index("gy") & 1]).astype(jnp.int32)
    half = jax.ShapeDtypeStruct((planes, 16, width), F32)
    group = jax.ShapeDtypeStruct((planes, 8, width), F32)
    whole = jax.ShapeDtypeStruct(estimate.shape, F32)
    tables = (order, extents, psf_z, psf_y, psf_x)
    radii = (extents[:, 0] - 1) // 2
    sizes = sum((radii > r).astype(jnp.int32) for r in REACHES[:-1]) if len(REACHES) > 1 else jnp.zeros_like(radii)
    places = 2 * jnp.arange(views, dtype=jnp.int32)[:, None]
    chosen = order[:, None] == jnp.arange(views, dtype=jnp.int32)[None, :]
    packed = jnp.sum(jnp.where(chosen, sizes[None, :] << places, 0))
    state = call(split_kernel, [SMEM_SPEC, ANY_SPEC], [group, group, half], 1, [pltpu.SemaphoreType.DMA((3,))])(
        parity, estimate)
    passes = [functools.partial(view_pass, r, (group, half), parity, tables, measured) for r in reaches]

    def step(index, state):
        pos = jnp.reshape(index, (1,)).astype(jnp.int32)
        if len(passes) == 1:
            return (state[0],) + tuple(passes[0](pos, *state[1:]))
        return (state[0] >> 2,) + tuple(lax.switch(state[0] & 3, passes, pos, *state[1:]))

    state = lax.fori_loop(0, views, step, (packed, *state))[1:]
    return call(merge_kernel, [SMEM_SPEC] + [VMEM_SPEC] * 3, [whole], 1)(parity, *state)[0]


def solution(mesh):
    return jax.shard_map(
        on_device,
        mesh=mesh,
        in_specs=(P("gz", "gy", None), P(None, "gz", "gy", None), P(), P(), P(), P(), P()),
        out_specs=P("gz", "gy", None),
        check_vma=False,
    )
```
